32 devices in a mesh: rep: 4 (over x, core), fsdp: 8 (over z, y).
Axes of the slice: x: 2, y: 2, z: 4, core: 2. Of those that a mesh axis runs over, the one named last changes fastest.
Arguments:
- deltas: float32 [4, 1048576], P('rep', 'fsdp'), may hold values from -45 to 45
- noise_first: float32 [4, 1048576], P('rep', 'fsdp'), may hold values from 0 to 1
- params: float32 [1048576], P('fsdp'), may hold values from -6 to 6
- momentum: float32 [1048576], P('fsdp'), may hold values from -6 to 6
- noise_second: float32 [1048576], P('fsdp'), may hold values from 0 to 1
Outputs:
- new_params: float32 [1048576], P('fsdp')
- new_momentum: float32 [1048576], P('fsdp')
The draws below stay inside these ranges and needn't reach their ends.
All inputs are finite; a program needn't handle non-finite values.
Results may differ from the reference program's by a relative error of at most 0.0003.
Values may be sent and summed in bfloat16 or wider, within the bound.
A program may use at most 64 MiB of HBM per device.

```python
import jax
import jax.numpy as jnp
import numpy as np
from jax import lax

PARAM_DEV = 131072
BLOCK = 32
LEVELS = 8
REPLICAS = 4
PARAMS = 1048576


def draw_deltas(key, part):
    block_key, own_key, common_key, mixing_key, height_key = jax.random.split(jax.random.fold_in(key, 11), 5)
    shard_count = PARAMS // PARAM_DEV
    block_count = PARAMS // BLOCK
    block_scale = jnp.exp(jax.random.uniform(block_key, (block_count,), jnp.float32) * jnp.log(10.0))
    block_scale = jnp.repeat(block_scale, BLOCK)
    ramp_up = 3.0 ** (jnp.arange(PARAMS, dtype=jnp.float32) / PARAMS)
    heights = jnp.exp(jax.random.uniform(height_key, (shard_count,), jnp.float32) * jnp.log(3.0))
    height_rows = jnp.repeat(heights, PARAM_DEV)
    common_part = jnp.clip(jax.random.normal(common_key, (1, PARAMS), jnp.float32), -5.0, 5.0)
    mixing = jax.random.uniform(mixing_key, (shard_count,), jnp.float32, 0.0, 1.0)
    own_part = jnp.clip(jax.random.normal(own_key, (REPLICAS, PARAMS), jnp.float32), -5.0, 5.0)
    mixing_rows = jnp.repeat(mixing, PARAM_DEV)[None, :]
    base_draw = jnp.clip(mixing_rows * common_part + jnp.sqrt(1.0 - mixing_rows * mixing_rows) * own_part, -5.0, 5.0)
    scale_rows = block_scale * ramp_up * height_rows
    return (0.1 * base_draw * scale_rows[None, :]).astype(jnp.float32)


def shard_levels(rng, shape, cuts, smallest, high):
    factor_of, own = 1.0, jax.random.fold_in(rng, 6)
    for axis_at, parts in cuts:
        steps = jnp.exp(jax.random.uniform(jax.random.fold_in(own, axis_at), (parts,), jnp.float32, smallest / len(cuts), high / len(cuts)))
        factor_of = factor_of * jnp.repeat(steps, shape[axis_at] // parts).reshape([-1 if axis == axis_at else 1 for axis in range(len(shape))])
    return factor_of


def centred(key, extent, scale, limit, cuts=(), kind=jnp.bfloat16):
    loudness = shard_levels(key, extent, cuts, -0.22, 0.18) if cuts else 1.0
    result = jax.random.normal(key, extent, jnp.float32) * scale * loudness
    return jnp.minimum(jnp.maximum(result, -limit), limit).astype(kind)


def setup_inputs(seed: int = 0) -> dict:
    splits = jax.random.split(jax.random.key(seed), 6)
    return {
        "deltas": draw_deltas(jax.random.fold_in(splits[5], 71), 0),
        "noise_first": jnp.clip(1.0 * jax.random.uniform(splits[1], (REPLICAS, PARAMS), jnp.float32) ** shard_levels(splits[1], (REPLICAS, PARAMS), ((0, 4), (1, 8)), -0.2, 0.2), 0.0, 1.0),
        "params": centred(splits[2], (PARAMS,), 1.0, 6.0, ((0, 8),), jnp.float32),
        "momentum": centred(splits[3], (PARAMS,), 1.0, 6.0, ((0, 8),), jnp.float32),
        "noise_second": jnp.clip(1.0 * jax.random.uniform(splits[4], (PARAMS,), jnp.float32) ** shard_levels(splits[4], (PARAMS,), ((0, 8),), -0.2, 0.2), 0.0, 1.0),
    }


power_list = np.array([2.0 ** k for k in range(-40, 12)], dtype=np.float32)
target_rms = 0.2
outer_rate = 0.7
outer_mu = 0.9

def quantize(values, jitter):
    initial = values.shape
    blocks = values.reshape(-1, BLOCK)
    shaken = jitter.reshape(-1, BLOCK).astype(values.dtype)
    largest = lax.optimization_barrier(jnp.max(jnp.abs(blocks), axis=1, keepdims=True))
    powers = jnp.asarray(power_list, values.dtype)[None, :]
    ceiling = lax.optimization_barrier(jnp.max(jnp.where(powers < largest, 2.0 * powers, powers[:, :1]), axis=1, keepdims=True))
    scaled = blocks * (LEVELS / ceiling)
    lower = jnp.floor(scaled)
    bumped = jnp.where(scaled - lower > shaken, 1.0, 0.0).astype(values.dtype)
    return ((lower + bumped) * (ceiling / LEVELS)).reshape(initial)

def apply_update(outer_grad, params, momentum, mean_square):
    factor = target_rms / jnp.sqrt(mean_square + 1e-06)
    update = factor * outer_grad
    new_moment = outer_mu * momentum + update
    new_param = params - outer_rate * (update + outer_mu * new_moment)
    return (new_param, new_moment)

def reference(deltas, noise_first, params, momentum, noise_second):

    def accumulate(running, pair):
        return (running + quantize(pair[0], pair[1]), None)
    summed, ignored = lax.scan(accumulate, jnp.zeros((deltas.shape[1],), deltas.dtype), (deltas, noise_first))
    average = summed / REPLICAS
    outer_grad = quantize(average, noise_second)
    return apply_update(outer_grad, params, momentum, jnp.mean(outer_grad * outer_grad))
```

```python
import functools

import jax
import jax.numpy as jnp
from jax import lax
from jax.experimental import pallas as pl
from jax.experimental.pallas import tpu as pltpu
from jax.sharding import PartitionSpec as P

MESH = pl.DeviceIdType.MESH
LANES = 128
BLOCK = 32
LEVELS = 8
SMALLEST = 2.0**-40
UNDER = 1.0 - 2.0**-24
target_rms = 0.2
outer_rate = 0.7
outer_mu = 0.9


def block_max(values):
    lane = lax.broadcasted_iota(jnp.int32, values.shape, 1)
    largest = jnp.abs(values)
    step = 1
    while step < BLOCK:
        ahead = pltpu.roll(largest, LANES - step, 1)
        behind = pltpu.roll(largest, step, 1)
        largest = jnp.maximum(largest, jnp.where((lane & step) != 0, behind, ahead))
        step *= 2
    return largest


def quantize(values, jitter):
    largest = jnp.maximum(block_max(values), SMALLEST)
    spread = (largest * UNDER) * ((2.0**24 + 2.0) / LEVELS)
    unit = spread - spread * UNDER
    magic = unit * (1.5 * 2.0**23)
    near = (values + magic) - magic
    lower = jnp.where(near > values, near - unit, near)
    return lower + jnp.where(values - lower > jitter * unit, unit, 0.0)


def kernel(reps, fsdps, chunks, x_hbm, u_hbm, p_hbm, m_hbm, w_hbm, newp_hbm, newm_hbm,
           xv, uv, wv, pv, mv, snd, own, got, pair, gmine, gother, sq,
           x_sem, u_sem, w_sem, p_sem, m_sem, op_sem, om_sem,
           s1, r1, s2, r2, s3, r3, s4, r4):
    rep, fsdp = lax.axis_index("rep"), lax.axis_index("fsdp")
    core, chip = lax.rem(rep, 2), rep // 2
    partner = rep + 1 - 2 * core
    chips, sources = reps // 2, 2 * fsdps
    half = xv.shape[1]
    rows = half // chunks
    me = fsdp * 2 + core

    def chip_peer(d):
        other = lax.rem(chip + d, chips)
        return other, (2 * other + core, fsdp)

    def sum_peer(d):
        other = lax.rem(me + d, sources)
        return other, (rep - core + lax.rem(other, 2), other // 2)

    barrier = pltpu.get_barrier_semaphore()
    for d in range(1, chips):
        pl.semaphore_signal(barrier, inc=1, device_id=chip_peer(d)[1], device_id_type=MESH)

    def greet(d, carry):
        pl.semaphore_signal(barrier, inc=1, device_id=sum_peer(d)[1], device_id_type=MESH)
        return carry

    lax.fori_loop(1, sources, greet, 0)

    starts = ((1 - core) * half, core * half)

    def piece(start, c):
        return pl.ds(pl.multiple_of(start + c * rows, rows), rows)

    def part(c):
        return pl.ds(c * rows, rows)

    x_in, u_in = {}, {}
    for s in (0, 1):
        for c in range(chunks):
            x_in[s, c] = pltpu.make_async_copy(
                x_hbm.at[piece(starts[s], c)], xv.at[s, part(c)], x_sem.at[s, c])
            u_in[s, c] = pltpu.make_async_copy(
                u_hbm.at[piece(starts[s], c)], uv.at[s, part(c)], u_sem.at[s, c])
            x_in[s, c].start()
            u_in[s, c].start()
    mine = pl.ds(pl.multiple_of(starts[1], half), half)
    w_in = pltpu.make_async_copy(w_hbm.at[mine], wv, w_sem)
    w_in.start()
    p_in, m_in = {}, {}
    for s in (1, 0):
        span = pl.ds(pl.multiple_of(starts[s], half), half)
        m_in[s] = pltpu.make_async_copy(m_hbm.at[span], mv.at[s], m_sem.at[s])
        p_in[s] = pltpu.make_async_copy(p_hbm.at[span], pv.at[s], p_sem.at[s])
        m_in[s].start()
        p_in[s].start()

    first = []
    for c in range(chunks):
        x_in[0, c].wait()
        u_in[0, c].wait()
        snd[part(c)] = quantize(xv[0, part(c)], uv[0, part(c)]).astype(jnp.bfloat16)
        if c == 0:
            pl.semaphore_wait(barrier, chips - 1 + sources - 1)
        copy = pltpu.make_async_remote_copy(
            snd.at[part(c)], got.at[part(c)], s1.at[c], r1.at[c],
            device_id=(partner, fsdp), device_id_type=MESH)
        copy.start()
        first.append(copy)
    for c in range(chunks):
        x_in[1, c].wait()
        u_in[1, c].wait()
        own[part(c)] = quantize(xv[1, part(c)], uv[1, part(c)])

    second = []
    for c in range(chunks):
        first[c].wait_recv()
        both = own[part(c)] + got[part(c)].astype(jnp.float32)
        pair[chip, part(c)] = both.astype(jnp.bfloat16)
        for d in range(1, chips):
            copy = pltpu.make_async_remote_copy(
                pair.at[chip, part(c)], pair.at[chip, part(c)],
                s2.at[d, c], r2.at[chip, c],
                device_id=chip_peer(d)[1], device_id_type=MESH)
            copy.start()
            second.append(copy)

    for s in (1, 0):
        m_in[s].wait()
        p_in[s].wait()
        pv[s] = pv[s] - (outer_rate * outer_mu * outer_mu) * mv[s]
        mv[s] = outer_mu * mv[s]

    w_in.wait()
    third = []
    squares = jnp.zeros((8, LANES), jnp.float32)
    for c in range(chunks):
        for d in range(1, chips):
            other, where = chip_peer(d)
            pltpu.make_async_remote_copy(
                pair.at[other, part(c)], pair.at[other, part(c)],
                s2.at[d, c], r2.at[other, c],
                device_id=where, device_id_type=MESH).wait_recv()
        total = pair[0, part(c)].astype(jnp.float32)
        for k in range(1, chips):
            total = total + pair[k, part(c)].astype(jnp.float32)
        grad = quantize(total / reps, wv[part(c)])
        gmine[part(c)] = grad.astype(jnp.bfloat16)
        copy = pltpu.make_async_remote_copy(
            gmine.at[part(c)], gother.at[part(c)], s3.at[c], r3.at[c],
            device_id=(partner, fsdp), device_id_type=MESH)
        copy.start()
        third.append(copy)
        squares = squares + jnp.sum((grad * grad).reshape(-1, 8, LANES), axis=0)

    sq[me] = jnp.sum(squares, axis=0, keepdims=True)

    def tell(d, carry):
        pltpu.make_async_remote_copy(
            sq.at[me], sq.at[me], s4.at[d], r4.at[me],
            device_id=sum_peer(d)[1], device_id_type=MESH).start()
        return carry

    lax.fori_loop(1, sources, tell, 0)

    def hear(d, carry):
        other, where = sum_peer(d)
        pltpu.make_async_remote_copy(
            sq.at[other], sq.at[other], s4.at[d], r4.at[other],
            device_id=where, device_id_type=MESH).wait_recv()
        return carry

    lax.fori_loop(1, sources, hear, 0)
    mean_square = jnp.sum(jnp.sum(sq[...], axis=0), axis=1, keepdims=True) / (2 * half * LANES * fsdps)
    factor = target_rms / jnp.sqrt(mean_square + 1e-06)
    slope = (outer_rate * (1.0 + outer_mu)) * factor

    outs = []
    for s, grads in ((1, gmine), (0, gother)):
        for c in range(chunks):
            if s == 0:
                third[c].wait_recv()
            grad = grads[part(c)].astype(jnp.float32)
            mv[s, part(c)] = mv[s, part(c)] + factor * grad
            pv[s, part(c)] = pv[s, part(c)] - slope * grad
            for v, out, sem in ((mv, newm_hbm, om_sem), (pv, newp_hbm, op_sem)):
                copy = pltpu.make_async_copy(
                    v.at[s, part(c)], out.at[piece(starts[s], c)], sem.at[s, c])
                copy.start()
                outs.append(copy)

    for copy in first + second + third:
        copy.wait_send()

    def told(d, carry):
        pltpu.make_async_remote_copy(
            sq.at[me], sq.at[me], s4.at[d], r4.at[me],
            device_id=sum_peer(d)[1], device_id_type=MESH).wait_send()
        return carry

    lax.fori_loop(1, sources, told, 0)
    for copy in outs:
        copy.wait()


def local(reps, fsdps, deltas, noise_first, params, momentum, noise_second):
    size = params.shape[0]
    total_rows = size // LANES
    half = total_rows // 2
    chunks = next(c for c in (4, 2, 1) if half % (16 * c) == 0)
    chips, sources = reps // 2, 2 * fsdps
    shape = (total_rows, LANES)
    f32, bf16 = jnp.float32, jnp.bfloat16
    dma = pltpu.SemaphoreType.DMA
    hbm = pl.BlockSpec(memory_space=pl.ANY)
    out = jax.ShapeDtypeStruct(shape, f32)
    new_params, new_momentum = pl.pallas_call(
        functools.partial(kernel, reps, fsdps, chunks),
        out_shape=(out, out),
        in_specs=[hbm] * 5,
        out_specs=(hbm, hbm),
        scratch_shapes=[
            pltpu.VMEM((2, half, LANES), f32),
            pltpu.VMEM((2, half, LANES), f32),
            pltpu.VMEM((half, LANES), f32),
            pltpu.VMEM((2, half, LANES), f32),
            pltpu.VMEM((2, half, LANES), f32),
            pltpu.VMEM((half, LANES), bf16),
            pltpu.VMEM((half, LANES), f32),
            pltpu.VMEM((half, LANES), bf16),
            pltpu.VMEM((chips, half, LANES), bf16),
            pltpu.VMEM((half, LANES), bf16),
            pltpu.VMEM((half, LANES), bf16),
            pltpu.VMEM((sources, 1, LANES), f32),
            dma((2, chunks)), dma((2, chunks)), dma, dma((2,)), dma((2,)),
            dma((2, chunks)), dma((2, chunks)),
            dma((chunks,)), dma((chunks,)),
            dma((chips, chunks)), dma((chips, chunks)),
            dma((chunks,)), dma((chunks,)),
            dma((sources,)), dma((sources,)),
        ],
        compiler_params=pltpu.CompilerParams(collective_id=0, has_side_effects=True),
        name="outer_step",
    )(deltas.reshape(shape), noise_first.reshape(shape), params.reshape(shape),
      momentum.reshape(shape), noise_second.reshape(shape))
    return new_params.reshape(size), new_momentum.reshape(size)


def solution(mesh):
    in_specs = (P("rep", "fsdp"), P("rep", "fsdp"), P("fsdp"), P("fsdp"), P("fsdp"))
    out_specs = (P("fsdp"), P("fsdp"))
    body = functools.partial(local, mesh.shape["rep"], mesh.shape["fsdp"])
    return jax.shard_map(body, mesh=mesh, in_specs=in_specs, out_specs=out_specs, check_vma=False)
```

```python
import functools

import jax
import jax.numpy as jnp
from jax import lax
from jax.experimental import pallas as pl
from jax.experimental.pallas import tpu as pltpu
from jax.sharding import PartitionSpec as P

MESH = pl.DeviceIdType.MESH
LANES = 128
BLOCK = 32
LEVELS = 8
SMALLEST = 2.0**-40
UNDER = 1.0 - 2.0**-24
target_rms = 0.2
outer_rate = 0.7
outer_mu = 0.9


def block_max(values):
    lane = lax.broadcasted_iota(jnp.int32, values.shape, 1)
    largest = jnp.abs(values)
    step = 1
    while step < BLOCK:
        ahead = pltpu.roll(largest, LANES - step, 1)
        behind = pltpu.roll(largest, step, 1)
        largest = jnp.maximum(largest, jnp.where((lane & step) != 0, behind, ahead))
        step *= 2
    return largest


def quantize(values, jitter):
    largest = jnp.maximum(block_max(values), SMALLEST)
    spread = (largest * UNDER) * ((2.0**24 + 2.0) / LEVELS)
    unit = spread - spread * UNDER
    magic = unit * (1.5 * 2.0**23)
    near = (values + magic) - magic
    lower = jnp.where(near > values, near - unit, near)
    return lower + jnp.where(values - lower > jitter * unit, unit, 0.0)


def gather(reps, fsdps, chunks, x_hbm, u_hbm, p_hbm, m_hbm, w_hbm, pv, mv, grads, sq,
           xv, uv, wv, snd, own, got, pair,
           x_sem, u_sem, w_sem, p_sem, m_sem, s1, r1, s2, r2, s3, r3, s4, r4, hands):
    rep, fsdp = lax.axis_index("rep"), lax.axis_index("fsdp")
    core, chip = lax.rem(rep, 2), rep // 2
    partner = rep + 1 - 2 * core
    chips, sources = reps // 2, 2 * fsdps
    half = xv.shape[1]
    rows = half // chunks
    me = fsdp * 2 + core

    def chip_peer(d):
        other = lax.rem(chip + d, chips)
        return other, (2 * other + core, fsdp)

    def sum_peer(d):
        other = lax.rem(me + d, sources)
        return other, (rep - core + lax.rem(other, 2), other // 2)

    barrier = pltpu.get_barrier_semaphore()
    for d in range(1, chips):
        pl.semaphore_signal(barrier, inc=1, device_id=chip_peer(d)[1], device_id_type=MESH)

    bits = (sources - 1).bit_length()

    def cube_peer(k):
        other = me + (1 - 2 * lax.rem(me // 2**k, 2)) * 2**k
        return (rep - core + lax.rem(other, 2), other // 2)

    for k in range(bits):
        pl.semaphore_signal(barrier, inc=1, device_id=cube_peer(k), device_id_type=MESH)

    def pass_on(k):
        pl.semaphore_signal(hands.at[k], inc=1, device_id=cube_peer(k), device_id_type=MESH)

    def take_in(k):
        pl.semaphore_wait(hands.at[k], 1)

    starts = ((1 - core) * half, core * half)

    def piece(start, c):
        return pl.ds(pl.multiple_of(start + c * rows, rows), rows)

    def part(c):
        return pl.ds(c * rows, rows)

    x_in, u_in = {}, {}
    for s in (0, 1):
        for c in range(chunks):
            x_in[s, c] = pltpu.make_async_copy(
                x_hbm.at[piece(starts[s], c)], xv.at[s, part(c)], x_sem.at[s, c])
            u_in[s, c] = pltpu.make_async_copy(
                u_hbm.at[piece(starts[s], c)], uv.at[s, part(c)], u_sem.at[s, c])
            x_in[s, c].start()
            u_in[s, c].start()
    mine = pl.ds(pl.multiple_of(starts[1], half), half)
    w_in = pltpu.make_async_copy(w_hbm.at[mine], wv, w_sem)
    w_in.start()
    p_in, m_in = {}, {}
    for s in (1, 0):
        span = pl.ds(pl.multiple_of(starts[s], half), half)
        m_in[s] = pltpu.make_async_copy(m_hbm.at[span], mv.at[s], m_sem.at[s])
        p_in[s] = pltpu.make_async_copy(p_hbm.at[span], pv.at[s], p_sem.at[s])
        m_in[s].start()
        p_in[s].start()

    first = []
    for c in range(chunks):
        x_in[0, c].wait()
        u_in[0, c].wait()
        snd[part(c)] = quantize(xv[0, part(c)], uv[0, part(c)]).astype(jnp.bfloat16)
        if c == 0:
            pl.semaphore_wait(barrier, chips - 1 + bits)
        copy = pltpu.make_async_remote_copy(
            snd.at[part(c)], got.at[part(c)], s1.at[c], r1.at[c],
            device_id=(partner, fsdp), device_id_type=MESH)
        copy.start()
        first.append(copy)
    pass_on(bits - 1)
    for c in range(chunks):
        x_in[1, c].wait()
        u_in[1, c].wait()
        own[part(c)] = quantize(xv[1, part(c)], uv[1, part(c)])

    second = []
    for c in range(chunks):
        first[c].wait_recv()
        both = own[part(c)] + got[part(c)].astype(jnp.float32)
        pair[chip, part(c)] = both.astype(jnp.bfloat16)
        for d in range(1, chips):
            copy = pltpu.make_async_remote_copy(
                pair.at[chip, part(c)], pair.at[chip, part(c)],
                s2.at[d, c], r2.at[chip, c],
                device_id=chip_peer(d)[1], device_id_type=MESH)
            copy.start()
            second.append(copy)

    for s in (1, 0):
        take_in(bits - 1) if s == 1 else None
        pass_on(bits - 2) if s == 1 else None
        m_in[s].wait()
        p_in[s].wait()
        pv[s] = pv[s] - (outer_rate * outer_mu * outer_mu) * mv[s]
        mv[s] = outer_mu * mv[s]

    w_in.wait()
    for k in range(bits - 2, -1, -1):
        take_in(k)
        if k:
            pass_on(k - 1)
    third = []
    squares = jnp.zeros((8, LANES), jnp.float32)
    for c in range(chunks):
        for d in range(1, chips):
            other, where = chip_peer(d)
            pltpu.make_async_remote_copy(
                pair.at[other, part(c)], pair.at[other, part(c)],
                s2.at[d, c], r2.at[other, c],
                device_id=where, device_id_type=MESH).wait_recv()
        total = pair[0, part(c)].astype(jnp.float32)
        for k in range(1, chips):
            total = total + pair[k, part(c)].astype(jnp.float32)
        grad = quantize(total / reps, wv[part(c)])
        grads[1, part(c)] = grad.astype(jnp.bfloat16)
        copy = pltpu.make_async_remote_copy(
            grads.at[1, part(c)], grads.at[0, part(c)], s3.at[c], r3.at[c],
            device_id=(partner, fsdp), device_id_type=MESH)
        copy.start()
        third.append(copy)
        squares = squares + jnp.sum((grad * grad).reshape(-1, 8, LANES), axis=0)

    sq[me] = jnp.sum(squares, axis=0, keepdims=True)

    def tell(d, carry):
        pltpu.make_async_remote_copy(
            sq.at[me], sq.at[me], s4.at[d], r4.at[me],
            device_id=sum_peer(d)[1], device_id_type=MESH).start()
        return carry

    lax.fori_loop(1, sources, tell, 0)

    def hear(d, carry):
        other, where = sum_peer(d)
        pltpu.make_async_remote_copy(
            sq.at[other], sq.at[other], s4.at[d], r4.at[other],
            device_id=where, device_id_type=MESH).wait_recv()
        return carry

    lax.fori_loop(1, sources, hear, 0)
    for copy in third:
        copy.wait_recv()
    for copy in first + second + third:
        copy.wait_send()

    def told(d, carry):
        pltpu.make_async_remote_copy(
            sq.at[me], sq.at[me], s4.at[d], r4.at[me],
            device_id=sum_peer(d)[1], device_id_type=MESH).wait_send()
        return carry

    lax.fori_loop(1, sources, told, 0)


def finish(count, chunks, pv, mv, grads, sq, newp_hbm, newm_hbm, op, om, op_sem, om_sem):
    core = lax.rem(lax.axis_index("rep"), 2)
    half = pv.shape[1]
    rows = half // chunks
    mean_square = jnp.sum(jnp.sum(sq[...], axis=0), axis=1, keepdims=True) / count
    factor = target_rms / jnp.sqrt(mean_square + 1e-06)
    slope = (outer_rate * (1.0 + outer_mu)) * factor
    outs = []
    for s, start in ((1, core * half), (0, (1 - core) * half)):
        for c in range(chunks):
            part = pl.ds(c * rows, rows)
            grad = grads[s, part].astype(jnp.float32)
            om[s, part] = mv[s, part] + factor * grad
            op[s, part] = pv[s, part] - slope * grad
            piece = pl.ds(pl.multiple_of(start + c * rows, rows), rows)
            for v, out, sem in ((om, newm_hbm, om_sem), (op, newp_hbm, op_sem)):
                copy = pltpu.make_async_copy(v.at[s, part], out.at[piece], sem.at[s, c])
                copy.start()
                outs.append(copy)
    for copy in outs:
        copy.wait()


def local(reps, fsdps, deltas, noise_first, params, momentum, noise_second):
    size = params.shape[0]
    total_rows = size // LANES
    half = total_rows // 2
    chunks = next(c for c in (2, 1) if half % (16 * c) == 0)
    chips, sources = reps // 2, 2 * fsdps
    shape = (total_rows, LANES)
    f32, bf16 = jnp.float32, jnp.bfloat16
    dma = pltpu.SemaphoreType.DMA
    hbm = pl.BlockSpec(memory_space=pl.ANY)
    vmem = pl.BlockSpec(memory_space=pltpu.VMEM)
    out = jax.ShapeDtypeStruct(shape, f32)
    halves = (2, half, LANES)
    parts = pl.pallas_call(
        functools.partial(gather, reps, fsdps, chunks),
        out_shape=(pltpu.VMEM(halves, f32), pltpu.VMEM(halves, f32),
                   pltpu.VMEM(halves, bf16), pltpu.VMEM((sources, 1, LANES), f32)),
        in_specs=[hbm] * 5,
        out_specs=(vmem,) * 4,
        scratch_shapes=[
            pltpu.VMEM(halves, f32),
            pltpu.VMEM(halves, f32),
            pltpu.VMEM((half, LANES), f32),
            pltpu.VMEM((half, LANES), bf16),
            pltpu.VMEM((half, LANES), f32),
            pltpu.VMEM((half, LANES), bf16),
            pltpu.VMEM((chips, half, LANES), bf16),
            dma((2, chunks)), dma((2, chunks)), dma, dma((2,)), dma((2,)),
            dma((chunks,)), dma((chunks,)),
            dma((chips, chunks)), dma((chips, chunks)),
            dma((chunks,)), dma((chunks,)),
            dma((sources,)), dma((sources,)),
            pltpu.SemaphoreType.REGULAR(((sources - 1).bit_length(),)),
        ],
        compiler_params=pltpu.CompilerParams(collective_id=0, has_side_effects=True),
        name="gather_step",
    )(deltas.reshape(shape), noise_first.reshape(shape), params.reshape(shape),
      momentum.reshape(shape), noise_second.reshape(shape))
    new_params, new_momentum = pl.pallas_call(
        functools.partial(finish, size * fsdps, chunks),
        out_shape=(out, out),
        in_specs=[vmem] * 4,
        out_specs=(hbm, hbm),
        scratch_shapes=[pltpu.VMEM(halves, f32), pltpu.VMEM(halves, f32),
                        dma((2, chunks)), dma((2, chunks))],
        name="finish_step",
    )(*[pltpu.with_memory_space_constraint(p, pltpu.VMEM) for p in parts])
    return new_params.reshape(size), new_momentum.reshape(size)


def solution(mesh):
    in_specs = (P("rep", "fsdp"), P("rep", "fsdp"), P("fsdp"), P("fsdp"), P("fsdp"))
    out_specs = (P("fsdp"), P("fsdp"))
    body = functools.partial(local, mesh.shape["rep"], mesh.shape["fsdp"])
    return jax.shard_map(body, mesh=mesh, in_specs=in_specs, out_specs=out_specs, check_vma=False)
```

```python
import functools

import jax
import jax.numpy as jnp
from jax import lax
from jax.experimental import pallas as pl
from jax.experimental.pallas import tpu as pltpu
from jax.sharding import PartitionSpec as P

MESH = pl.DeviceIdType.MESH
LANES = 128
BLOCK = 32
LEVELS = 8
SMALLEST = 2.0**-40
UNDER = 1.0 - 2.0**-24
target_rms = 0.2
outer_rate = 0.7
outer_mu = 0.9


def block_max(values):
    lane = lax.broadcasted_iota(jnp.int32, values.shape, 1)
    largest = jnp.abs(values)
    step = 1
    while step < BLOCK:
        ahead = pltpu.roll(largest, LANES - step, 1)
        behind = pltpu.roll(largest, step, 1)
        largest = jnp.maximum(largest, jnp.where((lane & step) != 0, behind, ahead))
        step *= 2
    return largest


def quantize(values, jitter):
    largest = jnp.maximum(block_max(values), SMALLEST)
    spread = (largest * UNDER) * ((2.0**24 + 2.0) / LEVELS)
    unit = spread - spread * UNDER
    magic = unit * (1.5 * 2.0**23)
    near = (values + magic) - magic
    lower = jnp.where(near > values, near - unit, near)
    return lower + jnp.where(values - lower > jitter * unit, unit, 0.0)


def gather(reps, fsdps, chunks, x_hbm, u_hbm, p_hbm, m_hbm, w_hbm, pv, mv, grads, sq,
           xv, uv, wv, snd, own, got, pair,
           x_sem, u_sem, w_sem, p_sem, m_sem, s1, r1, s2, r2, s3, r3, s4, r4, hands):
    rep, fsdp = lax.axis_index("rep"), lax.axis_index("fsdp")
    core, chip = lax.rem(rep, 2), rep // 2
    partner = rep + 1 - 2 * core
    chips, sources = reps // 2, 2 * fsdps
    half = xv.shape[1]
    rows = half // chunks
    me = fsdp * 2 + core

    def chip_peer(d):
        other = lax.rem(chip + d, chips)
        return other, (2 * other + core, fsdp)

    def sum_peer(d):
        other = lax.rem(me + d, sources)
        return other, (rep - core + lax.rem(other, 2), other // 2)

    barrier = pltpu.get_barrier_semaphore()
    for d in range(1, chips):
        pl.semaphore_signal(barrier, inc=1, device_id=chip_peer(d)[1], device_id_type=MESH)

    bits = (sources - 1).bit_length()

    def cube_peer(k):
        other = me + (1 - 2 * lax.rem(me // 2**k, 2)) * 2**k
        return (rep - core + lax.rem(other, 2), other // 2)

    for k in range(bits):
        pl.semaphore_signal(barrier, inc=1, device_id=cube_peer(k), device_id_type=MESH)

    def pass_on(k):
        pl.semaphore_signal(hands.at[k], inc=1, device_id=cube_peer(k), device_id_type=MESH)

    def take_in(k):
        pl.semaphore_wait(hands.at[k], 1)

    starts = ((1 - core) * half, core * half)

    def piece(start, c):
        return pl.ds(pl.multiple_of(start + c * rows, rows), rows)

    def part(c):
        return pl.ds(c * rows, rows)

    x_in, u_in = {}, {}
    for s in (0, 1):
        for c in range(chunks):
            x_in[s, c] = pltpu.make_async_copy(
                x_hbm.at[piece(starts[s], c)], xv.at[s, part(c)], x_sem.at[s, c])
            u_in[s, c] = pltpu.make_async_copy(
                u_hbm.at[piece(starts[s], c)], uv.at[s, part(c)], u_sem.at[s, c])
            x_in[s, c].start()
            u_in[s, c].start()
    mine = pl.ds(pl.multiple_of(starts[1], half), half)
    w_in = pltpu.make_async_copy(w_hbm.at[mine], wv, w_sem)
    w_in.start()
    p_in, m_in = {}, {}
    for s in (1, 0):
        span = pl.ds(pl.multiple_of(starts[s], half), half)
        m_in[s] = pltpu.make_async_copy(m_hbm.at[span], mv.at[s], m_sem.at[s])
        p_in[s] = pltpu.make_async_copy(p_hbm.at[span], pv.at[s], p_sem.at[s])
        m_in[s].start()
        p_in[s].start()

    first = []
    for c in range(chunks):
        x_in[0, c].wait()
        u_in[0, c].wait()
        snd[part(c)] = quantize(xv[0, part(c)], uv[0, part(c)]).astype(jnp.bfloat16)
        if c == 0:
            pl.semaphore_wait(barrier, chips - 1 + bits)
        copy = pltpu.make_async_remote_copy(
            snd.at[part(c)], got.at[part(c)], s1.at[c], r1.at[c],
            device_id=(partner, fsdp), device_id_type=MESH)
        copy.start()
        first.append(copy)
    pass_on(bits - 1)
    for c in range(chunks):
        x_in[1, c].wait()
        u_in[1, c].wait()
        own[part(c)] = quantize(xv[1, part(c)], uv[1, part(c)])

    second = []
    for c in range(chunks):
        first[c].wait_recv()
        both = own[part(c)] + got[part(c)].astype(jnp.float32)
        pair[chip, part(c)] = both.astype(jnp.bfloat16)
        for d in range(1, chips):
            copy = pltpu.make_async_remote_copy(
                pair.at[chip, part(c)], pair.at[chip, part(c)],
                s2.at[d, c], r2.at[chip, c],
                device_id=chip_peer(d)[1], device_id_type=MESH)
            copy.start()
            second.append(copy)

    for s in (1, 0):
        take_in(bits - 1) if s == 1 else None
        pass_on(bits - 2) if s == 1 else None
        m_in[s].wait()
        p_in[s].wait()
        pv[s] = pv[s] - (outer_rate * outer_mu * outer_mu) * mv[s]
        mv[s] = outer_mu * mv[s]

    w_in.wait()
    for k in range(bits - 2, -1, -1):
        take_in(k)
        if k:
            pass_on(k - 1)
    third = []
    squares = jnp.zeros((8, LANES), jnp.float32)
    for c in range(chunks):
        for d in range(1, chips):
            other, where = chip_peer(d)
            pltpu.make_async_remote_copy(
                pair.at[other, part(c)], pair.at[other, part(c)],
                s2.at[d, c], r2.at[other, c],
                device_id=where, device_id_type=MESH).wait_recv()
        total = pair[0, part(c)].astype(jnp.float32)
        for k in range(1, chips):
            total = total + pair[k, part(c)].astype(jnp.float32)
        grad = quantize(total / reps, wv[part(c)])
        grads[1, part(c)] = grad.astype(jnp.bfloat16)
        copy = pltpu.make_async_remote_copy(
            grads.at[1, part(c)], grads.at[0, part(c)], s3.at[c], r3.at[c],
            device_id=(partner, fsdp), device_id_type=MESH)
        copy.start()
        third.append(copy)
        squares = squares + jnp.sum((grad * grad).reshape(-1, 8, LANES), axis=0)

    sq[me] = jnp.sum(squares, axis=0, keepdims=True)

    for d in range(1, sources):
        pltpu.make_async_remote_copy(
            sq.at[me], sq.at[me], s4, r4,
            device_id=sum_peer(d)[1], device_id_type=MESH).start()
    others = sq.at[pl.ds(0, sources - 1)]
    sums = pltpu.make_async_remote_copy(
        others, others, s4, r4, device_id=(partner, fsdp), device_id_type=MESH)
    for copy in third:
        copy.wait_recv()
    for copy in first + second + third:
        copy.wait_send()
    sums.wait_recv()
    sums.wait_send()


def finish(count, chunks, pv, mv, grads, sq, newp_hbm, newm_hbm, op, om, op_sem, om_sem):
    core = lax.rem(lax.axis_index("rep"), 2)
    half = pv.shape[1]
    rows = half // chunks
    mean_square = jnp.sum(jnp.sum(sq[...], axis=0), axis=1, keepdims=True) / count
    factor = target_rms / jnp.sqrt(mean_square + 1e-06)
    slope = (outer_rate * (1.0 + outer_mu)) * factor
    outs = []
    for s, start in ((1, core * half), (0, (1 - core) * half)):
        for c in range(chunks):
            part = pl.ds(c * rows, rows)
            grad = grads[s, part].astype(jnp.float32)
            om[s, part] = mv[s, part] + factor * grad
            op[s, part] = pv[s, part] - slope * grad
            piece = pl.ds(pl.multiple_of(start + c * rows, rows), rows)
            for v, out, sem in ((om, newm_hbm, om_sem), (op, newp_hbm, op_sem)):
                copy = pltpu.make_async_copy(v.at[s, part], out.at[piece], sem.at[s, c])
                copy.start()
                outs.append(copy)
    for copy in outs:
        copy.wait()


def local(reps, fsdps, deltas, noise_first, params, momentum, noise_second):
    size = params.shape[0]
    total_rows = size // LANES
    half = total_rows // 2
    chunks = next(c for c in (2, 1) if half % (16 * c) == 0)
    chips, sources = reps // 2, 2 * fsdps
    shape = (total_rows, LANES)
    f32, bf16 = jnp.float32, jnp.bfloat16
    dma = pltpu.SemaphoreType.DMA
    hbm = pl.BlockSpec(memory_space=pl.ANY)
    vmem = pl.BlockSpec(memory_space=pltpu.VMEM)
    out = jax.ShapeDtypeStruct(shape, f32)
    halves = (2, half, LANES)
    parts = pl.pallas_call(
        functools.partial(gather, reps, fsdps, chunks),
        out_shape=(pltpu.VMEM(halves, f32), pltpu.VMEM(halves, f32),
                   pltpu.VMEM(halves, bf16), pltpu.VMEM((sources, 1, LANES), f32)),
        in_specs=[hbm] * 5,
        out_specs=(vmem,) * 4,
        scratch_shapes=[
            pltpu.VMEM(halves, f32),
            pltpu.VMEM(halves, f32),
            pltpu.VMEM((half, LANES), f32),
            pltpu.VMEM((half, LANES), bf16),
            pltpu.VMEM((half, LANES), f32),
            pltpu.VMEM((half, LANES), bf16),
            pltpu.VMEM((chips, half, LANES), bf16),
            dma((2, chunks)), dma((2, chunks)), dma, dma((2,)), dma((2,)),
            dma((chunks,)), dma((chunks,)),
            dma((chips, chunks)), dma((chips, chunks)),
            dma((chunks,)), dma((chunks,)),
            dma, dma,
            pltpu.SemaphoreType.REGULAR(((sources - 1).bit_length(),)),
        ],
        compiler_params=pltpu.CompilerParams(collective_id=0, has_side_effects=True),
        name="gather_step",
    )(deltas.reshape(shape), noise_first.reshape(shape), params.reshape(shape),
      momentum.reshape(shape), noise_second.reshape(shape))
    new_params, new_momentum = pl.pallas_call(
        functools.partial(finish, size * fsdps, chunks),
        out_shape=(out, out),
        in_specs=[vmem] * 4,
        out_specs=(hbm, hbm),
        scratch_shapes=[pltpu.VMEM(halves, f32), pltpu.VMEM(halves, f32),
                        dma((2, chunks)), dma((2, chunks))],
        name="finish_step",
    )(*[pltpu.with_memory_space_constraint(p, pltpu.VMEM) for p in parts])
    return new_params.reshape(size), new_momentum.reshape(size)


def solution(mesh):
    in_specs = (P("rep", "fsdp"), P("rep", "fsdp"), P("fsdp"), P("fsdp"), P("fsdp"))
    out_specs = (P("fsdp"), P("fsdp"))
    body = functools.partial(local, mesh.shape["rep"], mesh.shape["fsdp"])
    return jax.shard_map(body, mesh=mesh, in_specs=in_specs, out_specs=out_specs, check_vma=False)
```

```python
import functools

import jax
import jax.numpy as jnp
from jax import lax
from jax.experimental import pallas as pl
from jax.experimental.pallas import tpu as pltpu
from jax.sharding import PartitionSpec as P

MESH = pl.DeviceIdType.MESH
LANES = 128
BLOCK = 32
LEVELS = 8
SMALLEST = 2.0**-40
UNDER = 1.0 - 2.0**-24
target_rms = 0.2
outer_rate = 0.7
outer_mu = 0.9


def quantize(values, jitter):
    rows = values.shape[0]
    turned = jnp.abs(values).T.reshape(LANES // BLOCK, BLOCK, rows)
    largest = jnp.maximum(jnp.max(turned, axis=1, keepdims=True), SMALLEST)
    spread = (largest * UNDER) * ((2.0**24 + 2.0) / LEVELS)
    unit = spread - spread * UNDER
    unit = jnp.broadcast_to(unit, turned.shape).reshape(LANES, rows).T
    magic = unit * (1.5 * 2.0**23)
    near = (values + magic) - magic
    lower = jnp.where(near > values, near - unit, near)
    return lower + jnp.where(values - lower > jitter * unit, unit, 0.0)


def gather(reps, fsdps, chunks, x_hbm, u_hbm, p_hbm, m_hbm, w_hbm, pv, mv, grads, sq,
           xv, uv, wv, snd, own, got, pair,
           x_sem, u_sem, w_sem, p_sem, m_sem, s1, r1, s2, r2, s3, r3, s4, r4, hands):
    rep, fsdp = lax.axis_index("rep"), lax.axis_index("fsdp")
    core, chip = lax.rem(rep, 2), rep // 2
    partner = rep + 1 - 2 * core
    chips, sources = reps // 2, 2 * fsdps
    half = xv.shape[1]
    rows = half // chunks
    me = fsdp * 2 + core

    def chip_peer(d):
        other = lax.rem(chip + d, chips)
        return other, (2 * other + core, fsdp)

    def sum_peer(d):
        other = lax.rem(me + d, sources)
        return other, (rep - core + lax.rem(other, 2), other // 2)

    barrier = pltpu.get_barrier_semaphore()
    for d in range(1, chips):
        pl.semaphore_signal(barrier, inc=1, device_id=chip_peer(d)[1], device_id_type=MESH)

    bits = (sources - 1).bit_length()

    def cube_peer(k):
        other = me + (1 - 2 * lax.rem(me // 2**k, 2)) * 2**k
        return (rep - core + lax.rem(other, 2), other // 2)

    for k in range(bits):
        pl.semaphore_signal(barrier, inc=1, device_id=cube_peer(k), device_id_type=MESH)

    def pass_on(k):
        pl.semaphore_signal(hands.at[k], inc=1, device_id=cube_peer(k), device_id_type=MESH)

    def take_in(k):
        pl.semaphore_wait(hands.at[k], 1)

    starts = ((1 - core) * half, core * half)

    def piece(start, c):
        return pl.ds(pl.multiple_of(start + c * rows, rows), rows)

    def part(c):
        return pl.ds(c * rows, rows)

    x_in, u_in = {}, {}
    for s in (0, 1):
        for c in range(chunks):
            x_in[s, c] = pltpu.make_async_copy(
                x_hbm.at[piece(starts[s], c)], xv.at[s, part(c)], x_sem.at[s, c])
            u_in[s, c] = pltpu.make_async_copy(
                u_hbm.at[piece(starts[s], c)], uv.at[s, part(c)], u_sem.at[s, c])
            x_in[s, c].start()
            u_in[s, c].start()
    mine = pl.ds(pl.multiple_of(starts[1], half), half)
    w_in = pltpu.make_async_copy(w_hbm.at[mine], wv, w_sem)
    w_in.start()
    p_in, m_in = {}, {}
    for s in (1, 0):
        span = pl.ds(pl.multiple_of(starts[s], half), half)
        m_in[s] = pltpu.make_async_copy(m_hbm.at[span], mv.at[s], m_sem.at[s])
        p_in[s] = pltpu.make_async_copy(p_hbm.at[span], pv.at[s], p_sem.at[s])
        m_in[s].start()
        p_in[s].start()

    first = []
    for c in range(chunks):
        x_in[0, c].wait()
        u_in[0, c].wait()
        snd[part(c)] = quantize(xv[0, part(c)], uv[0, part(c)]).astype(jnp.bfloat16)
        if c == 0:
            pl.semaphore_wait(barrier, chips - 1 + bits)
        copy = pltpu.make_async_remote_copy(
            snd.at[part(c)], got.at[part(c)], s1.at[c], r1.at[c],
            device_id=(partner, fsdp), device_id_type=MESH)
        copy.start()
        first.append(copy)
    pass_on(bits - 1)
    for c in range(chunks):
        x_in[1, c].wait()
        u_in[1, c].wait()
        own[part(c)] = quantize(xv[1, part(c)], uv[1, part(c)])

    second = []
    for c in range(chunks):
        first[c].wait_recv()
        both = own[part(c)] + got[part(c)].astype(jnp.float32)
        pair[chip, part(c)] = both.astype(jnp.bfloat16)
        for d in range(1, chips):
            copy = pltpu.make_async_remote_copy(
                pair.at[chip, part(c)], pair.at[chip, part(c)],
                s2.at[d, c], r2.at[chip, c],
                device_id=chip_peer(d)[1], device_id_type=MESH)
            copy.start()
            second.append(copy)

    for s in (1, 0):
        take_in(bits - 1) if s == 1 else None
        pass_on(bits - 2) if s == 1 else None
        m_in[s].wait()
        p_in[s].wait()
        pv[s] = pv[s] - (outer_rate * outer_mu * outer_mu) * mv[s]
        mv[s] = outer_mu * mv[s]

    w_in.wait()
    for k in range(bits - 2, -1, -1):
        take_in(k)
        if k:
            pass_on(k - 1)
    third = []
    squares = jnp.zeros((8, LANES), jnp.float32)
    for c in range(chunks):
        for d in range(1, chips):
            other, where = chip_peer(d)
            pltpu.make_async_remote_copy(
                pair.at[other, part(c)], pair.at[other, part(c)],
                s2.at[d, c], r2.at[other, c],
                device_id=where, device_id_type=MESH).wait_recv()
        total = pair[0, part(c)].astype(jnp.float32)
        for k in range(1, chips):
            total = total + pair[k, part(c)].astype(jnp.float32)
        grad = quantize(total / reps, wv[part(c)])
        grads[1, part(c)] = grad.astype(jnp.bfloat16)
        copy = pltpu.make_async_remote_copy(
            grads.at[1, part(c)], grads.at[0, part(c)], s3.at[c], r3.at[c],
            device_id=(partner, fsdp), device_id_type=MESH)
        copy.start()
        third.append(copy)
        squares = squares + jnp.sum((grad * grad).reshape(-1, 8, LANES), axis=0)

    sq[me] = jnp.sum(squares, axis=0, keepdims=True)

    for d in range(1, sources):
        pltpu.make_async_remote_copy(
            sq.at[me], sq.at[me], s4, r4,
            device_id=sum_peer(d)[1], device_id_type=MESH).start()
    others = sq.at[pl.ds(0, sources - 1)]
    sums = pltpu.make_async_remote_copy(
        others, others, s4, r4, device_id=(partner, fsdp), device_id_type=MESH)
    for copy in third:
        copy.wait_recv()
    for copy in first + second + third:
        copy.wait_send()
    sums.wait_recv()
    sums.wait_send()


def finish(count, chunks, pv, mv, grads, sq, newp_hbm, newm_hbm, op, om, op_sem, om_sem):
    core = lax.rem(lax.axis_index("rep"), 2)
    half = pv.shape[1]
    rows = half // chunks
    mean_square = jnp.sum(jnp.sum(sq[...], axis=0), axis=1, keepdims=True) / count
    factor = target_rms / jnp.sqrt(mean_square + 1e-06)
    slope = (outer_rate * (1.0 + outer_mu)) * factor
    outs = []
    for s, start in ((1, core * half), (0, (1 - core) * half)):
        for c in range(chunks):
            part = pl.ds(c * rows, rows)
            grad = grads[s, part].astype(jnp.float32)
            om[s, part] = mv[s, part] + factor * grad
            op[s, part] = pv[s, part] - slope * grad
            piece = pl.ds(pl.multiple_of(start + c * rows, rows), rows)
            for v, out, sem in ((om, newm_hbm, om_sem), (op, newp_hbm, op_sem)):
                copy = pltpu.make_async_copy(v.at[s, part], out.at[piece], sem.at[s, c])
                copy.start()
                outs.append(copy)
    for copy in outs:
        copy.wait()


def local(reps, fsdps, deltas, noise_first, params, momentum, noise_second):
    size = params.shape[0]
    total_rows = size // LANES
    half = total_rows // 2
    chunks = next(c for c in (2, 1) if half % (16 * c) == 0)
    chips, sources = reps // 2, 2 * fsdps
    shape = (total_rows, LANES)
    f32, bf16 = jnp.float32, jnp.bfloat16
    dma = pltpu.SemaphoreType.DMA
    hbm = pl.BlockSpec(memory_space=pl.ANY)
    vmem = pl.BlockSpec(memory_space=pltpu.VMEM)
    out = jax.ShapeDtypeStruct(shape, f32)
    halves = (2, half, LANES)
    parts = pl.pallas_call(
        functools.partial(gather, reps, fsdps, chunks),
        out_shape=(pltpu.VMEM(halves, f32), pltpu.VMEM(halves, f32),
                   pltpu.VMEM(halves, bf16), pltpu.VMEM((sources, 1, LANES), f32)),
        in_specs=[hbm] * 5,
        out_specs=(vmem,) * 4,
        scratch_shapes=[
            pltpu.VMEM(halves, f32),
            pltpu.VMEM(halves, f32),
            pltpu.VMEM((half, LANES), f32),
            pltpu.VMEM((half, LANES), bf16),
            pltpu.VMEM((half, LANES), f32),
            pltpu.VMEM((half, LANES), bf16),
            pltpu.VMEM((chips, half, LANES), bf16),
            dma((2, chunks)), dma((2, chunks)), dma, dma((2,)), dma((2,)),
            dma((chunks,)), dma((chunks,)),
            dma((chips, chunks)), dma((chips, chunks)),
            dma((chunks,)), dma((chunks,)),
            dma, dma,
            pltpu.SemaphoreType.REGULAR(((sources - 1).bit_length(),)),
        ],
        compiler_params=pltpu.CompilerParams(collective_id=0, has_side_effects=True),
        name="gather_step",
    )(deltas.reshape(shape), noise_first.reshape(shape), params.reshape(shape),
      momentum.reshape(shape), noise_second.reshape(shape))
    new_params, new_momentum = pl.pallas_call(
        functools.partial(finish, size * fsdps, chunks),
        out_shape=(out, out),
        in_specs=[vmem] * 4,
        out_specs=(hbm, hbm),
        scratch_shapes=[pltpu.VMEM(halves, f32), pltpu.VMEM(halves, f32),
                        dma((2, chunks)), dma((2, chunks))],
        name="finish_step",
    )(*[pltpu.with_memory_space_constraint(p, pltpu.VMEM) for p in parts])
    return new_params.reshape(size), new_momentum.reshape(size)


def solution(mesh):
    in_specs = (P("rep", "fsdp"), P("rep", "fsdp"), P("fsdp"), P("fsdp"), P("fsdp"))
    out_specs = (P("fsdp"), P("fsdp"))
    body = functools.partial(local, mesh.shape["rep"], mesh.shape["fsdp"])
    return jax.shard_map(body, mesh=mesh, in_specs=in_specs, out_specs=out_specs, check_vma=False)
```

```python
import functools

import jax
import jax.numpy as jnp
from jax import lax
from jax.experimental import pallas as pl
from jax.experimental.pallas import tpu as pltpu
from jax.sharding import PartitionSpec as P

MESH = pl.DeviceIdType.MESH
LANES = 128
BLOCK = 32
LEVELS = 8
SMALLEST = 2.0**-40
UNDER = 1.0 - 2.0**-24
target_rms = 0.2
outer_rate = 0.7
outer_mu = 0.9


def quantize(values, jitter):
    rows = values.shape[0]
    turned = jnp.abs(values).T.reshape(LANES // BLOCK, BLOCK, rows)
    largest = jnp.maximum(jnp.max(turned, axis=1, keepdims=True), SMALLEST)
    spread = (largest * UNDER) * ((2.0**24 + 2.0) / LEVELS)
    unit = spread - spread * UNDER
    unit = jnp.broadcast_to(unit, turned.shape).reshape(LANES, rows).T
    magic = unit * (1.5 * 2.0**23)
    near = (values + magic) - magic
    lower = jnp.where(near > values, near - unit, near)
    return lower + jnp.where(values - lower > jitter * unit, unit, 0.0)


def gather(reps, fsdps, chunks, x_hbm, u_hbm, p_hbm, m_hbm, w_hbm, pv, mv, grads, sq,
           xv, uv, wv, snd, own, got, pair, raw,
           x_sem, u_sem, w_sem, p_sem, m_sem, s1, r1, s2, r2, s3, r3, s4, r4, s5, r5, hands):
    rep, fsdp = lax.axis_index("rep"), lax.axis_index("fsdp")
    core, chip = lax.rem(rep, 2), rep // 2
    partner = rep + 1 - 2 * core
    chips, sources = reps // 2, 2 * fsdps
    half = xv.shape[1]
    rows = half // chunks
    me = fsdp * 2 + core

    def chip_peer(d):
        other = lax.rem(chip + d, chips)
        return other, (2 * other + core, fsdp)

    def sum_peer(d):
        other = lax.rem(me + d, sources)
        return other, (rep - core + lax.rem(other, 2), other // 2)

    barrier = pltpu.get_barrier_semaphore()
    for d in range(1, chips):
        other, where = chip_peer(d)
        pl.semaphore_signal(barrier, inc=1, device_id=where, device_id_type=MESH)
        pl.semaphore_signal(barrier, inc=1, device_id=(2 * other + 1 - core, fsdp), device_id_type=MESH)

    bits = (sources - 1).bit_length()

    def cube_peer(k):
        other = me + (1 - 2 * lax.rem(me // 2**k, 2)) * 2**k
        return (rep - core + lax.rem(other, 2), other // 2)

    for k in range(bits):
        pl.semaphore_signal(barrier, inc=1, device_id=cube_peer(k), device_id_type=MESH)

    def pass_on(k):
        pl.semaphore_signal(hands.at[k], inc=1, device_id=cube_peer(k), device_id_type=MESH)

    def take_in(k):
        pl.semaphore_wait(hands.at[k], 1)

    starts = ((1 - core) * half, core * half)

    def piece(start, c):
        return pl.ds(pl.multiple_of(start + c * rows, rows), rows)

    def part(c):
        return pl.ds(c * rows, rows)

    x_in, u_in = {}, {}
    for s in (0, 1):
        for c in range(chunks):
            x_in[s, c] = pltpu.make_async_copy(
                x_hbm.at[piece(starts[s], c)], xv.at[s, part(c)], x_sem.at[s, c])
            u_in[s, c] = pltpu.make_async_copy(
                u_hbm.at[piece(starts[s], c)], uv.at[s, part(c)], u_sem.at[s, c])
            x_in[s, c].start()
            u_in[s, c].start()
    mine = pl.ds(pl.multiple_of(starts[1], half), half)
    w_in = pltpu.make_async_copy(w_hbm.at[mine], wv, w_sem)
    w_in.start()
    p_in, m_in = {}, {}
    for s in (1, 0):
        span = pl.ds(pl.multiple_of(starts[s], half), half)
        m_in[s] = pltpu.make_async_copy(m_hbm.at[span], mv.at[s], m_sem.at[s])
        p_in[s] = pltpu.make_async_copy(p_hbm.at[span], pv.at[s], p_sem.at[s])
        m_in[s].start()
        p_in[s].start()

    straight = []

    def send_straight(source, k, cores):
        copy = pltpu.make_async_remote_copy(
            source, raw.at[rep], s5.at[len(straight)], r5.at[rep],
            device_id=(2 * k + cores, fsdp), device_id_type=MESH)
        copy.start()
        straight.append(copy)

    x_in[0, 0].wait()
    u_in[0, 0].wait()
    snd[part(0)] = quantize(xv[0, part(0)], uv[0, part(0)]).astype(jnp.bfloat16)
    pl.semaphore_wait(barrier, 2 * (chips - 1) + bits)
    for d in range(chips):
        send_straight(snd.at[part(0)], lax.rem(chip + d, chips), 1 - core)
    x_in[1, 0].wait()
    u_in[1, 0].wait()
    raw[rep] = quantize(xv[1, part(0)], uv[1, part(0)]).astype(jnp.bfloat16)
    for d in range(1, chips):
        send_straight(raw.at[rep], lax.rem(chip + d, chips), core)

    first = []
    for c in range(1, chunks):
        x_in[0, c].wait()
        u_in[0, c].wait()
        snd[part(c)] = quantize(xv[0, part(c)], uv[0, part(c)]).astype(jnp.bfloat16)
        copy = pltpu.make_async_remote_copy(
            snd.at[part(c)], got.at[part(c)], s1.at[c], r1.at[c],
            device_id=(partner, fsdp), device_id_type=MESH)
        copy.start()
        first.append(copy)
    pass_on(bits - 1)
    for c in range(1, chunks):
        x_in[1, c].wait()
        u_in[1, c].wait()
        own[part(c)] = quantize(xv[1, part(c)], uv[1, part(c)])

    second = []
    for c in range(1, chunks):
        first[c - 1].wait_recv()
        both = own[part(c)] + got[part(c)].astype(jnp.float32)
        pair[chip, part(c)] = both.astype(jnp.bfloat16)
        for d in range(1, chips):
            copy = pltpu.make_async_remote_copy(
                pair.at[chip, part(c)], pair.at[chip, part(c)],
                s2.at[d, c], r2.at[chip, c],
                device_id=chip_peer(d)[1], device_id_type=MESH)
            copy.start()
            second.append(copy)

    for s in (1, 0):
        take_in(bits - 1) if s == 1 else None
        pass_on(bits - 2) if s == 1 else None
        m_in[s].wait()
        p_in[s].wait()
        pv[s] = pv[s] - (outer_rate * outer_mu * outer_mu) * mv[s]
        mv[s] = outer_mu * mv[s]

    w_in.wait()
    third = []
    squares = jnp.zeros((8, LANES), jnp.float32)
    for c in range(chunks):
        if c == 0:
            for d in range(1, reps):
                source = lax.rem(rep + d, reps)
                pltpu.make_async_remote_copy(
                    raw.at[source], raw.at[source], s5.at[0], r5.at[source],
                    device_id=(source, fsdp), device_id_type=MESH).wait_recv()
            total = raw[0].astype(jnp.float32)
            for k in range(1, reps):
                total = total + raw[k].astype(jnp.float32)
        else:
            for d in range(1, chips):
                other, where = chip_peer(d)
                pltpu.make_async_remote_copy(
                    pair.at[other, part(c)], pair.at[other, part(c)],
                    s2.at[d, c], r2.at[other, c],
                    device_id=where, device_id_type=MESH).wait_recv()
            total = pair[0, part(c)].astype(jnp.float32)
            for k in range(1, chips):
                total = total + pair[k, part(c)].astype(jnp.float32)
        grad = quantize(total / reps, wv[part(c)])
        grads[1, part(c)] = grad.astype(jnp.bfloat16)
        copy = pltpu.make_async_remote_copy(
            grads.at[1, part(c)], grads.at[0, part(c)], s3.at[c], r3.at[c],
            device_id=(partner, fsdp), device_id_type=MESH)
        copy.start()
        third.append(copy)
        if c == 0:
            for k in range(bits - 2, -1, -1):
                take_in(k)
                if k:
                    pass_on(k - 1)
        squares = squares + jnp.sum((grad * grad).reshape(-1, 8, LANES), axis=0)

    sq[me] = jnp.sum(squares, axis=0, keepdims=True)

    for d in range(1, sources):
        pltpu.make_async_remote_copy(
            sq.at[me], sq.at[me], s4, r4,
            device_id=sum_peer(d)[1], device_id_type=MESH).start()
    others = sq.at[pl.ds(0, sources - 1)]
    sums = pltpu.make_async_remote_copy(
        others, others, s4, r4, device_id=(partner, fsdp), device_id_type=MESH)
    for copy in third:
        copy.wait_recv()
    for copy in straight + first + second + third:
        copy.wait_send()
    sums.wait_recv()
    sums.wait_send()


def finish(count, chunks, pv, mv, grads, sq, newp_hbm, newm_hbm, op, om, op_sem, om_sem):
    core = lax.rem(lax.axis_index("rep"), 2)
    half = pv.shape[1]
    rows = half // chunks
    mean_square = jnp.sum(jnp.sum(sq[...], axis=0), axis=1, keepdims=True) / count
    factor = target_rms / jnp.sqrt(mean_square + 1e-06)
    slope = (outer_rate * (1.0 + outer_mu)) * factor
    outs = []
    for s, start in ((1, core * half), (0, (1 - core) * half)):
        for c in range(chunks):
            part = pl.ds(c * rows, rows)
            grad = grads[s, part].astype(jnp.float32)
            om[s, part] = mv[s, part] + factor * grad
            op[s, part] = pv[s, part] - slope * grad
            piece = pl.ds(pl.multiple_of(start + c * rows, rows), rows)
            for v, out, sem in ((om, newm_hbm, om_sem), (op, newp_hbm, op_sem)):
                copy = pltpu.make_async_copy(v.at[s, part], out.at[piece], sem.at[s, c])
                copy.start()
                outs.append(copy)
    for copy in outs:
        copy.wait()


def local(reps, fsdps, deltas, noise_first, params, momentum, noise_second):
    size = params.shape[0]
    total_rows = size // LANES
    half = total_rows // 2
    chunks = next(c for c in (4, 2, 1) if half % (16 * c) == 0)
    chips, sources = reps // 2, 2 * fsdps
    shape = (total_rows, LANES)
    f32, bf16 = jnp.float32, jnp.bfloat16
    dma = pltpu.SemaphoreType.DMA
    hbm = pl.BlockSpec(memory_space=pl.ANY)
    vmem = pl.BlockSpec(memory_space=pltpu.VMEM)
    out = jax.ShapeDtypeStruct(shape, f32)
    halves = (2, half, LANES)
    parts = pl.pallas_call(
        functools.partial(gather, reps, fsdps, chunks),
        out_shape=(pltpu.VMEM(halves, f32), pltpu.VMEM(halves, f32),
                   pltpu.VMEM(halves, bf16), pltpu.VMEM((sources, 1, LANES), f32)),
        in_specs=[hbm] * 5,
        out_specs=(vmem,) * 4,
        scratch_shapes=[
            pltpu.VMEM(halves, f32),
            pltpu.VMEM(halves, f32),
            pltpu.VMEM((half, LANES), f32),
            pltpu.VMEM((half, LANES), bf16),
            pltpu.VMEM((half, LANES), f32),
            pltpu.VMEM((half, LANES), bf16),
            pltpu.VMEM((chips, half, LANES), bf16),
            pltpu.VMEM((reps, half // chunks, LANES), bf16),
            dma((2, chunks)), dma((2, chunks)), dma, dma((2,)), dma((2,)),
            dma((chunks,)), dma((chunks,)),
            dma((chips, chunks)), dma((chips, chunks)),
            dma((chunks,)), dma((chunks,)),
            dma, dma, dma((reps,)), dma((reps,)),
            pltpu.SemaphoreType.REGULAR(((sources - 1).bit_length(),)),
        ],
        compiler_params=pltpu.CompilerParams(collective_id=0, has_side_effects=True),
        name="gather_step",
    )(deltas.reshape(shape), noise_first.reshape(shape), params.reshape(shape),
      momentum.reshape(shape), noise_second.reshape(shape))
    new_params, new_momentum = pl.pallas_call(
        functools.partial(finish, size * fsdps, chunks),
        out_shape=(out, out),
        in_specs=[vmem] * 4,
        out_specs=(hbm, hbm),
        scratch_shapes=[pltpu.VMEM(halves, f32), pltpu.VMEM(halves, f32),
                        dma((2, chunks)), dma((2, chunks))],
        name="finish_step",
    )(*[pltpu.with_memory_space_constraint(p, pltpu.VMEM) for p in parts])
    return new_params.reshape(size), new_momentum.reshape(size)


def solution(mesh):
    in_specs = (P("rep", "fsdp"), P("rep", "fsdp"), P("fsdp"), P("fsdp"), P("fsdp"))
    out_specs = (P("fsdp"), P("fsdp"))
    body = functools.partial(local, mesh.shape["rep"], mesh.shape["fsdp"])
    return jax.shard_map(body, mesh=mesh, in_specs=in_specs, out_specs=out_specs, check_vma=False)
```

```python
import functools

import jax
import jax.numpy as jnp
from jax import lax
from jax.experimental import pallas as pl
from jax.experimental.pallas import tpu as pltpu
from jax.sharding import PartitionSpec as P

MESH = pl.DeviceIdType.MESH
LANES = 128
BLOCK = 32
LEVELS = 8
SMALLEST = 2.0**-40
UNDER = 1.0 - 2.0**-24
target_rms = 0.2
outer_rate = 0.7
outer_mu = 0.9


def quantize(values, jitter):
    rows = values.shape[0]
    turned = jnp.abs(values).T.reshape(LANES // BLOCK, BLOCK, rows)
    largest = jnp.maximum(jnp.max(turned, axis=1, keepdims=True), SMALLEST)
    spread = (largest * UNDER) * ((2.0**24 + 2.0) / LEVELS)
    unit = spread - spread * UNDER
    unit = jnp.broadcast_to(unit, turned.shape).reshape(LANES, rows).T
    magic = unit * (1.5 * 2.0**23)
    near = (values + magic) - magic
    lower = jnp.where(near > values, near - unit, near)
    return lower + jnp.where(values - lower > jitter * unit, unit, 0.0)


def gather(reps, fsdps, chunks, x_hbm, u_hbm, p_hbm, m_hbm, w_hbm, pv, mv, grads, sq,
           xv, uv, wv, snd, got, pair,
           x_sem, u_sem, w_sem, p_sem, m_sem, s1, r1, s2, r2, s3, r3, s4, r4, hands):
    rep, fsdp = lax.axis_index("rep"), lax.axis_index("fsdp")
    core, chip = lax.rem(rep, 2), rep // 2
    partner = rep + 1 - 2 * core
    chips, sources = reps // 2, 2 * fsdps
    half = xv.shape[1]
    rows = half // chunks
    me = fsdp * 2 + core

    def chip_peer(d):
        other = lax.rem(chip + d, chips)
        return other, (2 * other + core, fsdp)

    def sum_peer(d):
        other = lax.rem(me + d, sources)
        return other, (rep - core + lax.rem(other, 2), other // 2)

    barrier = pltpu.get_barrier_semaphore()
    for d in range(1, chips):
        pl.semaphore_signal(barrier, inc=1, device_id=chip_peer(d)[1], device_id_type=MESH)

    bits = (sources - 1).bit_length()

    def cube_peer(k):
        other = me + (1 - 2 * lax.rem(me // 2**k, 2)) * 2**k
        return (rep - core + lax.rem(other, 2), other // 2)

    for k in range(bits):
        pl.semaphore_signal(barrier, inc=1, device_id=cube_peer(k), device_id_type=MESH)

    def pass_on(k):
        pl.semaphore_signal(hands.at[k], inc=1, device_id=cube_peer(k), device_id_type=MESH)

    def take_in(k):
        pl.semaphore_wait(hands.at[k], 1)

    starts = ((1 - core) * half, core * half)

    def piece(start, c):
        return pl.ds(pl.multiple_of(start + c * rows, rows), rows)

    def part(c):
        return pl.ds(c * rows, rows)

    x_in, u_in = {}, {}
    for s in (0, 1):
        for c in range(chunks):
            x_in[s, c] = pltpu.make_async_copy(
                x_hbm.at[piece(starts[s], c)], xv.at[s, part(c)], x_sem.at[s, c])
            u_in[s, c] = pltpu.make_async_copy(
                u_hbm.at[piece(starts[s], c)], uv.at[s, part(c)], u_sem.at[s, c])
            x_in[s, c].start()
            u_in[s, c].start()
    mine = pl.ds(pl.multiple_of(starts[1], half), half)
    w_in = pltpu.make_async_copy(w_hbm.at[mine], wv, w_sem)
    w_in.start()
    p_in, m_in = {}, {}
    for s in (1, 0):
        span = pl.ds(pl.multiple_of(starts[s], half), half)
        m_in[s] = pltpu.make_async_copy(m_hbm.at[span], mv.at[s], m_sem.at[s])
        p_in[s] = pltpu.make_async_copy(p_hbm.at[span], pv.at[s], p_sem.at[s])
        m_in[s].start()
        p_in[s].start()

    first = []
    for c in range(chunks):
        x_in[0, c].wait()
        u_in[0, c].wait()
        snd[part(c)] = quantize(xv[0, part(c)], uv[0, part(c)]).astype(jnp.bfloat16)
        if c == 0:
            pl.semaphore_wait(barrier, chips - 1 + bits)
        copy = pltpu.make_async_remote_copy(
            snd.at[part(c)], got.at[part(c)], s1.at[c], r1.at[c],
            device_id=(partner, fsdp), device_id_type=MESH)
        copy.start()
        first.append(copy)
    pass_on(bits - 1)
    second = []
    for c in range(chunks):
        x_in[1, c].wait()
        u_in[1, c].wait()
        own = quantize(xv[1, part(c)], uv[1, part(c)])
        first[c].wait_recv()
        both = own + got[part(c)].astype(jnp.float32)
        pair[chip, part(c)] = both.astype(jnp.bfloat16)
        for d in range(1, chips):
            copy = pltpu.make_async_remote_copy(
                pair.at[chip, part(c)], pair.at[chip, part(c)],
                s2.at[d, c], r2.at[chip, c],
                device_id=chip_peer(d)[1], device_id_type=MESH)
            copy.start()
            second.append(copy)

    for s in (1, 0):
        take_in(bits - 1) if s == 1 else None
        pass_on(bits - 2) if s == 1 else None
        m_in[s].wait()
        p_in[s].wait()
        pv[s] = pv[s] - (outer_rate * outer_mu * outer_mu) * mv[s]
        mv[s] = outer_mu * mv[s]

    w_in.wait()
    third = []
    squares = jnp.zeros((8, LANES), jnp.float32)
    for c in range(chunks):
        for d in range(1, chips):
            other, where = chip_peer(d)
            pltpu.make_async_remote_copy(
                pair.at[other, part(c)], pair.at[other, part(c)],
                s2.at[d, c], r2.at[other, c],
                device_id=where, device_id_type=MESH).wait_recv()
        total = pair[0, part(c)].astype(jnp.float32)
        for k in range(1, chips):
            total = total + pair[k, part(c)].astype(jnp.float32)
        grad = quantize(total / reps, wv[part(c)])
        grads[1, part(c)] = grad.astype(jnp.bfloat16)
        copy = pltpu.make_async_remote_copy(
            grads.at[1, part(c)], grads.at[0, part(c)], s3.at[c], r3.at[c],
            device_id=(partner, fsdp), device_id_type=MESH)
        copy.start()
        third.append(copy)
        if c == 0:
            for k in range(bits - 2, -1, -1):
                take_in(k)
                if k:
                    pass_on(k - 1)
        squares = squares + jnp.sum((grad * grad).reshape(-1, 8, LANES), axis=0)

    sq[me] = jnp.sum(squares, axis=0, keepdims=True)

    for d in range(1, sources):
        pltpu.make_async_remote_copy(
            sq.at[me], sq.at[me], s4, r4,
            device_id=sum_peer(d)[1], device_id_type=MESH).start()
    others = sq.at[pl.ds(0, sources - 1)]
    sums = pltpu.make_async_remote_copy(
        others, others, s4, r4, device_id=(partner, fsdp), device_id_type=MESH)
    for copy in third:
        copy.wait_recv()
    for copy in first + second + third:
        copy.wait_send()
    sums.wait_recv()
    sums.wait_send()


def finish(count, chunks, pv, mv, grads, sq, newp_hbm, newm_hbm, op, om, op_sem, om_sem):
    core = lax.rem(lax.axis_index("rep"), 2)
    half = pv.shape[1]
    rows = half // chunks
    mean_square = jnp.sum(jnp.sum(sq[...], axis=0), axis=1, keepdims=True) / count
    factor = target_rms / jnp.sqrt(mean_square + 1e-06)
    slope = (outer_rate * (1.0 + outer_mu)) * factor
    outs = []
    for s, start in ((1, core * half), (0, (1 - core) * half)):
        for c in range(chunks):
            part = pl.ds(c * rows, rows)
            grad = grads[s, part].astype(jnp.float32)
            om[s, part] = mv[s, part] + factor * grad
            op[s, part] = pv[s, part] - slope * grad
            piece = pl.ds(pl.multiple_of(start + c * rows, rows), rows)
            for v, out, sem in ((om, newm_hbm, om_sem), (op, newp_hbm, op_sem)):
                copy = pltpu.make_async_copy(v.at[s, part], out.at[piece], sem.at[s, c])
                copy.start()
                outs.append(copy)
    for copy in outs:
        copy.wait()


def local(reps, fsdps, deltas, noise_first, params, momentum, noise_second):
    size = params.shape[0]
    total_rows = size // LANES
    half = total_rows // 2
    chunks = next(c for c in (2, 1) if half % (16 * c) == 0)
    chips, sources = reps // 2, 2 * fsdps
    shape = (total_rows, LANES)
    f32, bf16 = jnp.float32, jnp.bfloat16
    dma = pltpu.SemaphoreType.DMA
    hbm = pl.BlockSpec(memory_space=pl.ANY)
    vmem = pl.BlockSpec(memory_space=pltpu.VMEM)
    out = jax.ShapeDtypeStruct(shape, f32)
    halves = (2, half, LANES)
    parts = pl.pallas_call(
        functools.partial(gather, reps, fsdps, chunks),
        out_shape=(pltpu.VMEM(halves, f32), pltpu.VMEM(halves, f32),
                   pltpu.VMEM(halves, bf16), pltpu.VMEM((sources, 1, LANES), f32)),
        in_specs=[hbm] * 5,
        out_specs=(vmem,) * 4,
        scratch_shapes=[
            pltpu.VMEM(halves, f32),
            pltpu.VMEM(halves, f32),
            pltpu.VMEM((half, LANES), f32),
            pltpu.VMEM((half, LANES), bf16),
            pltpu.VMEM((half, LANES), bf16),
            pltpu.VMEM((chips, half, LANES), bf16),
            dma((2, chunks)), dma((2, chunks)), dma, dma((2,)), dma((2,)),
            dma((chunks,)), dma((chunks,)),
            dma((chips, chunks)), dma((chips, chunks)),
            dma((chunks,)), dma((chunks,)),
            dma, dma,
            pltpu.SemaphoreType.REGULAR(((sources - 1).bit_length(),)),
        ],
        compiler_params=pltpu.CompilerParams(collective_id=0, has_side_effects=True),
        name="gather_step",
    )(deltas.reshape(shape), noise_first.reshape(shape), params.reshape(shape),
      momentum.reshape(shape), noise_second.reshape(shape))
    new_params, new_momentum = pl.pallas_call(
        functools.partial(finish, size * fsdps, chunks),
        out_shape=(out, out),
        in_specs=[vmem] * 4,
        out_specs=(hbm, hbm),
        scratch_shapes=[pltpu.VMEM(halves, f32), pltpu.VMEM(halves, f32),
                        dma((2, chunks)), dma((2, chunks))],
        name="finish_step",
    )(*[pltpu.with_memory_space_constraint(p, pltpu.VMEM) for p in parts])
    return new_params.reshape(size), new_momentum.reshape(size)


def solution(mesh):
    in_specs = (P("rep", "fsdp"), P("rep", "fsdp"), P("fsdp"), P("fsdp"), P("fsdp"))
    out_specs = (P("fsdp"), P("fsdp"))
    body = functools.partial(local, mesh.shape["rep"], mesh.shape["fsdp"])
    return jax.shard_map(body, mesh=mesh, in_specs=in_specs, out_specs=out_specs, check_vma=False)
```
